256 devices in a mesh: dp: 16 (over z_lo, y), comp: 16 (over x, z_hi, core).
Axes of the slice: x: 4, y: 4, z: 8 (z_hi: 2, z_lo: 4; z = z_hi * 4 + z_lo), core: 2. Of those that a mesh axis runs over, the one named last changes fastest.
Arguments:
- points: bfloat16 [8192, 1024], P('dp'), may hold values from -6 to 6
- means: float32 [1024, 32768], P('dp', 'comp'), may hold values from -2.25 to 2.25
- variances: float32 [1024, 32768], P('dp', 'comp'), may hold values from 0.45 to 2.22
- log_weights: float32 [32768], P('comp'), may hold values from -4 to 4
- split_list: int32 [1024, 2], replicated, may hold values from 0 to 32767, as said below
- prune_list: int32 [1024], replicated, may hold values from 0 to 32767, as said below
Outputs:
- new_means: float32 [1024, 32768], P('dp', 'comp')
- new_variances: float32 [1024, 32768], P('dp', 'comp')
- new_log_weights: float32 [32768], P('comp')
The draws below stay inside these ranges and needn't reach their ends.
Inputs may be any that keep to these rules, and one draw needn't show every extreme that they name: `split_list`: rows j * 64 to (j + 1) * 64 - 1 of column 0 name 64 distinct components among j * 2048 to (j + 1) * 2048 - 1; column 1 is a permutation of 0 to 1023. `prune_list`: distinct components, none of them in column 0 of split_list, exactly 64 in each aligned block of 2048 ids.
All inputs are finite; a program needn't handle non-finite values.
Results may differ from the reference program's by a relative error of at most 0.004.
The reference program's roundings to bfloat16 on the way (of `x_sq` and `resp`) count: a program that leaves them out, or rounds other values in their place, can miss the bound.
Values may be sent and summed in bfloat16 or wider, within the bound.
No kernel may reach another device: no remote copies, remote signals or barrier semaphores. Data moves between devices by JAX's collectives and lax.ppermute only.
A program may use at most 64 MiB of HBM per device.

```python
import math
import jax
import jax.numpy as jnp
from jax import lax

D = 1024
K_DEV = 2048
SPL_DEV = 64
COMPONENTS = 32768
NPTS = 8192
SPLITS = 1024


def split_plan(key):
    base_key = jax.random.fold_in(key, 4242)
    blocks = COMPONENTS // K_DEV
    block_keys = jax.random.split(jax.random.fold_in(base_key, 1), blocks)
    orders = jax.vmap(lambda one_key: jax.random.permutation(one_key, K_DEV))(block_keys).astype(jnp.int32)
    orders = orders + (jnp.arange(blocks, dtype=jnp.int32) * K_DEV)[:, None]
    sources = orders[:, :SPL_DEV].reshape(-1)
    pruned = orders[:, SPL_DEV:2 * SPL_DEV].reshape(-1)
    shuffle = jax.random.permutation(jax.random.fold_in(base_key, 2), SPLITS).astype(jnp.int32)
    prune_order = pruned[shuffle]
    slot_index = jax.random.permutation(jax.random.fold_in(base_key, 3), SPLITS).astype(jnp.int32)
    return (jnp.stack([sources, slot_index], 1).astype(jnp.int32), prune_order.astype(jnp.int32))


def draw_split_list(key, part):
    return split_plan(key)[0]


def draw_prune_list(key, part):
    return split_plan(key)[1]


def perturbation(noise_key):
    noise = jnp.clip(jax.random.normal(noise_key, (D, COMPONENTS), jnp.float32), -5.0, 5.0)
    return noise


def draw_means(key, part):
    base_key = jax.random.fold_in(key, 7101)
    profile = jnp.clip(0.5 * jax.random.normal(jax.random.fold_in(base_key, 1), (D,), jnp.float32), -2.0, 2.0)
    noise = perturbation(jax.random.fold_in(base_key, 2))
    return profile[:, None] + 0.05 * noise


def draw_variances(key, part):
    base_key = jax.random.fold_in(key, 7202)
    low = math.log(0.5)
    high = math.log(2.0)
    profile = jax.random.uniform(jax.random.fold_in(base_key, 1), (D,), jnp.float32, low, high)
    noise = perturbation(jax.random.fold_in(base_key, 2))
    return jnp.exp(profile[:, None] + 0.02 * noise)


def levels(key, extent, cuts, least, largest):
    factor_of, own = 1.0, jax.random.fold_in(key, 6)
    for axis_at, blocks in cuts:
        steps = jnp.exp(jax.random.uniform(jax.random.fold_in(own, axis_at), (blocks,), jnp.float32, least / len(cuts), largest / len(cuts)))
        factor_of = factor_of * jnp.repeat(steps, extent[axis_at] // blocks).reshape([-1 if axis == axis_at else 1 for axis in range(len(extent))])
    return factor_of


def centred(stream_key, dims, width, most, pieces=(), kind=jnp.bfloat16):
    gain = levels(stream_key, dims, pieces, -0.22, 0.18) if pieces else 1.0
    drawn = jax.random.normal(stream_key, dims, jnp.float32) * width * gain
    return jnp.minimum(jnp.maximum(drawn, -most), most).astype(kind)


def setup_inputs(seed: int = 0) -> dict:
    arg_keys = jax.random.split(jax.random.key(seed), 7)
    points = centred(arg_keys[0], (NPTS, D), 1.0, 6.0, ((0, 16),))
    means = draw_means(jax.random.fold_in(arg_keys[6], 71), 0)
    variances = draw_variances(jax.random.fold_in(arg_keys[6], 71), 0)
    log_weights = centred(arg_keys[3], (COMPONENTS,), 1.0, 4.0, ((0, 16),), jnp.float32)
    split_list = draw_split_list(jax.random.fold_in(arg_keys[6], 71), 0)
    prune_list = draw_prune_list(jax.random.fold_in(arg_keys[6], 71), 0)
    return dict(points=points, means=means, variances=variances, log_weights=log_weights, split_list=split_list, prune_list=prune_list)


log_two_pi = math.log(2.0 * math.pi)
log_two = math.log(2.0)
prior_count = 1.0
split_scale = 0.5

def block_scores(points, x_sq, means_block, vars_block, weights_block):
    precision = 1.0 / vars_block
    prec_low = precision.astype(jnp.bfloat16)
    pm_low = (precision * means_block).astype(jnp.bfloat16)
    const = weights_block + 0.5 * lax.optimization_barrier(jnp.sum(jnp.log(precision), 0)) - 0.5 * lax.optimization_barrier(jnp.sum(precision * means_block * means_block, 0)) - 0.5 * D * log_two_pi
    quad = jnp.dot(x_sq, prec_low, preferred_element_type=jnp.float32)
    lin = jnp.dot(points, pm_low, preferred_element_type=jnp.float32)
    return -0.5 * quad + lin + const[None, :]

def reference(points, means, variances, log_weights, split_list, prune_list):
    blocks = COMPONENTS // K_DEV
    mean_blocks = means.reshape(D, blocks, K_DEV).transpose(1, 0, 2)
    var_blocks = variances.reshape(D, blocks, K_DEV).transpose(1, 0, 2)
    weight_blocks = log_weights.reshape(blocks, K_DEV)
    as_float = points.astype(jnp.float32)
    x_sq = (as_float * as_float).astype(jnp.bfloat16)

    def first_pass(operands):
        scores = block_scores(points, x_sq, operands[0], operands[1], operands[2])
        top = lax.optimization_barrier(jnp.max(scores, 1))
        return (top, lax.optimization_barrier(jnp.sum(jnp.exp(scores - top[:, None]), 1)))
    maxes, totals = lax.map(first_pass, (mean_blocks, var_blocks, weight_blocks))
    highest = lax.optimization_barrier(jnp.max(maxes, 0))
    lse = highest + jnp.log(lax.optimization_barrier(jnp.sum(totals * jnp.exp(maxes - highest[None, :]), 0)))
    contract = (((0,), (0,)), ((), ()))

    def second_pass(operands):
        scores = block_scores(points, x_sq, operands[0], operands[1], operands[2])
        resp = jnp.exp(scores - lse[:, None]).astype(jnp.bfloat16)
        counts = lax.optimization_barrier(jnp.sum(resp, 0, dtype=jnp.float32))
        sum_x = lax.dot_general(points, resp, contract, preferred_element_type=jnp.float32)
        sum_xx = lax.dot_general(x_sq, resp, contract, preferred_element_type=jnp.float32)
        return (counts, sum_x, sum_xx)
    counts, sum_x, sum_xx = lax.map(second_pass, (mean_blocks, var_blocks, weight_blocks))
    counts = counts.reshape(COMPONENTS)
    sum_x = sum_x.transpose(1, 0, 2).reshape(D, COMPONENTS)
    sum_xx = sum_xx.transpose(1, 0, 2).reshape(D, COMPONENTS)
    total = counts + prior_count
    mean_new = (sum_x + prior_count * means) / total[None, :]
    var_new = (sum_xx + prior_count * (variances + means * means)) / total[None, :] - mean_new * mean_new
    lw_new = jnp.log(total) - jnp.log(NPTS + COMPONENTS * prior_count)
    sources = split_list[:, 0]
    targets = prune_list[split_list[:, 1]]
    src_mean = mean_new[:, sources]
    src_var = var_new[:, sources]
    shift = split_scale * jnp.sqrt(src_var)
    new_means = mean_new.at[:, sources].add(shift)
    new_means = new_means.at[:, targets].set(src_mean - shift)
    new_variances = var_new.at[:, targets].set(src_var)
    src_weight = lw_new[sources] - log_two
    new_log_weights = lw_new.at[sources].set(src_weight)
    new_log_weights = new_log_weights.at[targets].set(src_weight)
    return (new_means, new_variances, new_log_weights)
```

```python
import functools
import math

import jax
import jax.numpy as jnp
from jax import lax
from jax.experimental import pallas as pl
from jax.experimental.pallas import tpu as pltpu
from jax.sharding import Mesh, PartitionSpec as P

log_two_pi = math.log(2.0 * math.pi)
log_two = math.log(2.0)
prior_count = 1.0
split_scale = 0.5
extra_rows = 8
count_rows = 16
f32 = jnp.float32
bf16 = jnp.bfloat16


DP = ("zl", "y")
COMP = ("x", "zh", "c")


def call(body, out_shape, name, cost, limit=40, **kw):
    return pl.pallas_call(
        body,
        out_shape=out_shape,
        name=name,
        cost_estimate=pl.CostEstimate(
            flops=cost[0], bytes_accessed=cost[1], transcendentals=0
        ),
        compiler_params=pltpu.CompilerParams(vmem_limit_bytes=limit << 20),
        **kw,
    )


def three(value):
    high = value.astype(bf16)
    rest = value - high.astype(f32)
    mid = rest.astype(bf16)
    low = (rest - mid.astype(f32)).astype(bf16)
    return high, mid, low


def prep_body(means_ref, variances_ref, out_ref):
    rows = means_ref.shape[0]
    precision = 1.0 / variances_ref[...]
    pm = precision * means_ref[...]
    out_ref[0, :rows, :] = pm.astype(bf16)
    out_ref[0, rows : 2 * rows, :] = -0.5 * precision.astype(bf16)
    partial = 0.5 * jnp.sum(jnp.log(precision), 0, keepdims=True) - 0.5 * jnp.sum(
        pm * means_ref[...], 0, keepdims=True
    )
    high, mid, low = three(partial)
    row = lax.broadcasted_iota(jnp.int32, (extra_rows, partial.shape[1]), 0)
    rest = jnp.where(
        row == 0,
        high.astype(f32),
        jnp.where(row == 1, mid.astype(f32), jnp.where(row == 2, low.astype(f32), 0.0)),
    )
    out_ref[0, 2 * rows :, :] = rest.astype(bf16)


def prep(means, variances, blocks):
    rows, cols = means.shape
    width = cols // blocks
    spec = pl.BlockSpec((rows, width), lambda i: (0, i))
    return call(
        prep_body,
        jax.ShapeDtypeStruct((blocks, 2 * rows + extra_rows, width), bf16),
        "prep",
        (rows * cols * 20, rows * cols * 12),
        grid=(blocks,),
        in_specs=[spec, spec],
        out_specs=pl.BlockSpec((1, 2 * rows + extra_rows, width), lambda i: (i, 0, 0)),
    )(means, variances)


def weights_body(y_ref, logw_ref, w0, w1, w2, w3, wt_ref, const_ref):
    parts = (w0, w1, w2, w3)
    n = len(parts)
    blocks, rows, width = w0.shape
    rows -= extra_rows
    const = logw_ref[...]
    for shift, part in enumerate(parts):
        source = lax.rem(y_ref[0] + (n - shift), n)
        for zl in range(blocks):
            start = pl.multiple_of((zl * n + source) * rows, rows)
            wt_ref[:, pl.ds(start, rows)] = part[zl, :rows, :].T
            extra = part[zl, rows:, :].astype(f32)
            const = const + (extra[0:1] + extra[1:2] + extra[2:3])
    const_ref[...] = jnp.broadcast_to(const, (128, width)).T


def weights(y, logw, parts):
    blocks, rows, width = parts[0].shape
    depth = blocks * len(parts) * (rows - extra_rows)
    smem = pl.BlockSpec(memory_space=pltpu.SMEM)
    vmem = pl.BlockSpec(memory_space=pltpu.VMEM)
    return call(
        weights_body,
        (
            jax.ShapeDtypeStruct((width, depth), bf16),
            jax.ShapeDtypeStruct((width, 128), f32),
        ),
        "weights",
        (depth * width, depth * width * 4),
        in_specs=[smem] + [vmem] * 5,
        out_specs=(vmem, vmem),
    )(y, logw, *parts)


def score_body(wt_ref, const_ref, xa_ref, xb_ref, score_ref, lse_ref, x2_ref):
    width = wt_ref.shape[0]
    const = const_ref[...]
    for half, ref in enumerate((xa_ref, xb_ref)):
        rows, features = ref.shape
        lane = lax.broadcasted_iota(jnp.int32, (rows, 128), 1)
        blocks = []
        for i in range(features // 128):
            x = ref[:, i * 128 : (i + 1) * 128].astype(f32)
            sq = (x * x).astype(bf16).astype(f32)
            first = jnp.where(lane < 64, x, pltpu.roll(sq, 64, 1)).astype(bf16)
            second = jnp.where(lane < 64, pltpu.roll(x, 64, 1), sq).astype(bf16)
            x2_ref[2 * i, half * rows : (half + 1) * rows, :] = first
            x2_ref[2 * i + 1, half * rows : (half + 1) * rows, :] = second
            blocks += [first, second]
        x2 = jnp.concatenate(blocks, axis=1)
        score = lax.dot_general(
            wt_ref[...], x2, (((1,), (1,)), ((), ())), preferred_element_type=f32
        )
        reps = -(-rows // 128)
        shift = jnp.concatenate([const] * reps, axis=1)[:, :rows]
        score = score + shift
        score_ref[:, half * rows : (half + 1) * rows] = score
        top = jnp.max(score, 0, keepdims=True)
        total = jnp.sum(jnp.exp(score - top), 0, keepdims=True)
        lse_ref[:, half * rows : (half + 1) * rows] = jnp.broadcast_to(
            top + jnp.log(total), (8, rows)
        )


def scores(wt, const, xa, xb):
    width, depth = wt.shape
    rows = xa.shape[0]
    vmem = pl.BlockSpec(memory_space=pltpu.VMEM)
    return call(
        score_body,
        (
            jax.ShapeDtypeStruct((width, 2 * rows), f32),
            jax.ShapeDtypeStruct((8, 2 * rows), f32),
            jax.ShapeDtypeStruct((depth // 128, 2 * rows, 128), bf16),
        ),
        "scores",
        (4 * width * depth * rows, width * depth * 2 + rows * depth * 6),
        in_specs=[vmem] * 4,
        out_specs=(vmem,) * 3,
    )(wt, const, xa, xb)


def resp_body(lse_ref, s0, s1, s2, s3, rt_ref, count_ref):
    parts = (s0, s1, s2, s3)
    width, rows = s0.shape
    total = jnp.zeros((width, 1), f32)
    for i, part in enumerate(parts):
        lse = lse_ref[0:1, i * rows : (i + 1) * rows]
        resp = jnp.exp(part[...] - lse).astype(bf16)
        rt_ref[:, i * rows : (i + 1) * rows] = resp
        total = total + jnp.sum(resp.astype(f32), 1, keepdims=True)
    count_ref[...] = jnp.broadcast_to(total, (width, 128)).T[0:8]


def resps(lse, parts):
    width, rows = parts[0].shape
    n = len(parts)
    vmem = pl.BlockSpec(memory_space=pltpu.VMEM)
    return call(
        resp_body,
        (
            jax.ShapeDtypeStruct((width, n * rows), bf16),
            jax.ShapeDtypeStruct((8, width), f32),
        ),
        "resps",
        (width * rows * n * 8, width * rows * n * 6),
        in_specs=[vmem] * 5,
        out_specs=(vmem,) * 2,
    )(lse, *parts)


def put_counts(count, out_ref, start):
    width = count.shape[1]
    pieces = []
    for part in three(count):
        for q in range(width // 128):
            pieces.append(part[:, q * 128 : (q + 1) * 128].astype(f32))
    pieces += [jnp.zeros((1, 128), f32)] * (count_rows - len(pieces))
    out_ref[start : start + count_rows, :] = jnp.concatenate(pieces, 0).astype(bf16)


def get_counts(rows, width):
    rows = rows.astype(f32)
    n = width // 128
    out = []
    for q in range(n):
        out.append(rows[q : q + 1] + rows[n + q : n + q + 1] + rows[2 * n + q : 2 * n + q + 1])
    return jnp.concatenate(out, axis=1)


def moment_body(ny, dest_ref, rt_ref, count_ref, a0, a1, a2, a3, out_ref):
    parts = (a0, a1, a2, a3)
    width = rt_ref.shape[0]
    rows = a0.shape[1]
    blocks = a0.shape[0] // ny
    acc = None
    for i, part in enumerate(parts):
        x2 = jnp.concatenate(
            [part[zl * ny + dest_ref[0]] for zl in range(blocks)], axis=1
        )
        one = jnp.dot(
            rt_ref[:, i * rows : (i + 1) * rows], x2, preferred_element_type=f32
        )
        acc = one if acc is None else acc + one
    for zl in range(blocks):
        out_ref[zl * width : (zl + 1) * width, :] = acc[
            :, zl * 128 : (zl + 1) * 128
        ].astype(bf16)
    put_counts(count_ref[0:1, :], out_ref, blocks * width)


def moments(dest, rt, count, parts, ny):
    width = rt.shape[0]
    blocks = parts[0].shape[0] // ny
    smem = pl.BlockSpec(memory_space=pltpu.SMEM)
    vmem = pl.BlockSpec(memory_space=pltpu.VMEM)
    return call(
        functools.partial(moment_body, ny),
        jax.ShapeDtypeStruct((blocks * width + count_rows, 128), bf16),
        "moments",
        (2 * rt.size * blocks * 128, rt.size * 2 + blocks * 128 * rt.shape[1] * 2),
        in_specs=[smem] + [vmem] * 6,
        out_specs=vmem,
    )(dest, rt, count, *parts)


def gather_body(p0, p1, p2, p3, out_ref):
    parts = (p0, p1, p2, p3)
    blocks = out_ref.shape[0]
    width = out_ref.shape[1] - count_rows
    count = None
    for part in parts:
        one = get_counts(part[blocks * width :, :], width)
        count = one if count is None else count + one
    for zl in range(blocks):
        acc = None
        for part in parts:
            one = part[zl * width : (zl + 1) * width, :].astype(f32)
            acc = one if acc is None else acc + one
        out_ref[zl, :width, :] = acc.astype(bf16)
        put_counts(count, out_ref.at[zl], width)


def gather(parts, blocks):
    width = (parts[0].shape[0] - count_rows) // blocks
    vmem = pl.BlockSpec(memory_space=pltpu.VMEM)
    return call(
        gather_body,
        jax.ShapeDtypeStruct((blocks, width + count_rows, 128), bf16),
        "gather",
        (parts[0].size * 4, parts[0].size * 10),
        in_specs=[vmem] * 4,
        out_specs=vmem,
    )(*parts)


def update_body(
    log_norm, sums_ref, means_ref, variances_ref, src_ref, mean_ref, var_ref, lw_ref, send_ref
):
    blocks = sums_ref.shape[0]
    width = sums_ref.shape[1] - count_rows
    rows = means_ref.shape[0]
    packed = None
    for zl in range(blocks):
        cols = slice(zl * width, (zl + 1) * width)
        sums = sums_ref[zl, :width, :].astype(f32).T
        total = get_counts(sums_ref[zl, width:, :], width) + prior_count
        inverse = 1.0 / total
        means = means_ref[:, cols]
        mean_new = (sums[:rows] + prior_count * means) * inverse
        var_new = (
            sums[rows:] + prior_count * (variances_ref[:, cols] + means * means)
        ) * inverse - mean_new * mean_new
        lw_new = jnp.log(total) - log_norm
        mean_ref[:, cols] = mean_new
        var_ref[:, cols] = var_new
        lw_ref[:, cols] = jnp.broadcast_to(lw_new, (8, width))
        moved = mean_new - split_scale * jnp.sqrt(var_new)
        high, mid, low = three(lw_new - log_two)
        row = lax.broadcasted_iota(jnp.int32, (extra_rows, width), 0)
        tail = jnp.where(
            row == 0,
            high.astype(f32),
            jnp.where(row == 1, mid.astype(f32), jnp.where(row == 2, low.astype(f32), 0.0)),
        )
        ids = lax.broadcasted_iota(jnp.int32, (width, 128), 0) + zl * width
        lane = lax.broadcasted_iota(jnp.int32, (width, 128), 1)
        hit = ids == src_ref[0:1, :]
        left = jnp.where(hit & (lane < 64), 1.0, 0.0).astype(bf16)
        right = jnp.where(hit & (lane >= 64), 1.0, 0.0).astype(bf16)
        first = jnp.concatenate([moved, tail], 0).astype(bf16)
        second = jnp.concatenate([var_new, jnp.zeros_like(tail)], 0).astype(bf16)
        one = jnp.dot(first, left, preferred_element_type=f32) + jnp.dot(
            second, right, preferred_element_type=f32
        )
        packed = one if packed is None else packed + one
    send_ref[...] = packed.astype(bf16)


def update(sums, means, variances, src, log_norm):
    rows, cols = means.shape
    vmem = pl.BlockSpec(memory_space=pltpu.VMEM)
    return call(
        functools.partial(update_body, log_norm),
        (
            jax.ShapeDtypeStruct((rows, cols), f32),
            jax.ShapeDtypeStruct((rows, cols), f32),
            jax.ShapeDtypeStruct((8, cols), f32),
            jax.ShapeDtypeStruct((rows + extra_rows, 128), bf16),
        ),
        "update",
        (rows * cols * 300, rows * cols * 20),
        in_specs=[vmem] * 4,
        out_specs=(vmem,) * 4,
    )(sums, means, variances, src)


def place_body(
    got_ref, target_ref, masks_ref, mean_ref, var_ref, lw_ref, out_mean, out_var, out_lw
):
    owners = got_ref.shape[0]
    rows = mean_ref.shape[0]
    lane = lax.broadcasted_iota(jnp.int32, got_ref.shape[1:], 1)
    firsts, seconds = [], []
    for j in range(0, owners, 2):
        one = got_ref[j].astype(f32)
        two = got_ref[j + 1].astype(f32)
        firsts.append(jnp.where(lane < 64, one, pltpu.roll(two, 64, 1)))
        seconds.append(jnp.where(lane < 64, pltpu.roll(one, 64, 1), two))
    left = jnp.concatenate(
        [jnp.concatenate(firsts, 1), jnp.concatenate(seconds, 1)], 0
    ).astype(bf16)
    placed = jnp.dot(left, target_ref[...], preferred_element_type=f32)
    take = masks_ref[0:1, :] > 0.5
    given = masks_ref[1:2, :]
    mean_new = mean_ref[...]
    var_new = var_ref[...]
    moved = mean_new + given * (split_scale * jnp.sqrt(var_new))
    out_mean[...] = jnp.where(take, placed[:rows], moved)
    base = rows + extra_rows
    out_var[...] = jnp.where(take, placed[base : base + rows], var_new)
    lw_placed = placed[rows : rows + 1] + placed[rows + 1 : rows + 2] + placed[rows + 2 : rows + 3]
    out_lw[...] = jnp.where(take, lw_placed, lw_ref[0:1, :] - log_two * given)


def place(got, target, masks, mean_new, var_new, lw_new):
    rows, cols = mean_new.shape
    vmem = pl.BlockSpec(memory_space=pltpu.VMEM)
    return call(
        place_body,
        (
            jax.ShapeDtypeStruct((rows, cols), f32),
            jax.ShapeDtypeStruct((rows, cols), f32),
            jax.ShapeDtypeStruct((1, cols), f32),
        ),
        "place",
        (300 * target.size, target.size * 2),
        in_specs=[vmem] * 6,
        out_specs=(vmem,) * 3,
    )(got, target, masks, mean_new, var_new, lw_new)


def swap(order, c):
    return jnp.where(c == 1, order[:, ::-1], order)


def flip(order, zl):
    n = order.shape[0]
    back = order[::-1]
    return lax.dynamic_slice_in_dim(
        jnp.concatenate([back, back], 0), n - 1 - zl, n, 0
    )


def per_device(points, means, variances, log_weights, split_list, prune_list):
    rows, k_dev = means.shape
    features = points.shape[1]
    n_rows = points.shape[0]
    nz = lax.axis_size("zl")
    ny = lax.axis_size("y")
    n_comp = lax.axis_size(COMP)
    zl = lax.axis_index("zl")
    y = lax.axis_index("y")
    c = lax.axis_index("c")
    comp = lax.axis_index(COMP)
    npts = n_rows * nz * ny
    n_components = k_dev * n_comp
    width = k_dev // nz
    half = n_rows // 2

    mine = lax.dynamic_slice_in_dim(points, c * half, half, 0)
    other = lax.dynamic_slice_in_dim(points, (1 - c) * half, half, 0)
    pieces = [(mine, other)]
    for s in range(1, nz):
        got = lax.ppermute(mine, "zl", [(i, (i + s) % nz) for i in range(nz)])
        pieces.append((got, lax.ppermute(got, "c", [(0, 1), (1, 0)])))

    packed = prep(means, variances, nz)
    packed = lax.all_to_all(packed, "zl", 0, 0, tiled=True)
    parts = [packed] + [
        lax.ppermute(packed, "y", [(i, (i + s) % ny) for i in range(ny)])
        for s in range(1, ny)
    ]
    logw = lax.dynamic_slice_in_dim(log_weights, zl * width, width, 0)
    logw = (logw - 0.5 * features * log_two_pi)[None, :]
    wt, const = weights(y.reshape(1).astype(jnp.int32), logw, parts)

    out = [scores(wt, const, a, b) for a, b in pieces]
    local = jnp.stack([o[1][0] for o in out]).reshape(nz, 2, half)
    local = flip(swap(local, c), zl).reshape(1, nz * n_rows)
    group = ("zl",) + COMP
    n_group = nz * n_comp
    every = lax.all_to_all(
        jnp.broadcast_to(local, (n_group, nz * n_rows)), group, 0, 0, tiled=True
    )
    top = jnp.max(every, 0)
    lse = top + jnp.log(jnp.sum(jnp.exp(every - top[None, :]), 0))
    lse = swap(flip(lse.reshape(nz, 2, half), zl), c).reshape(1, nz * n_rows)

    rt, count = resps(lse, [o[0] for o in out])
    x2 = [o[2] for o in out]
    sent = []
    order = list(range(1, ny)) + [0]
    for s in order:
        dest = lax.rem(y + s, ny).reshape(1).astype(jnp.int32)
        part = moments(dest, rt, count, x2, ny)
        if s:
            part = lax.ppermute(part, "y", [(i, (i + s) % ny) for i in range(ny)])
        sent.append(part)
    sums = gather(sent, nz)
    sums = lax.all_to_all(sums, "zl", 0, 0, tiled=True)

    spl = split_list.shape[0] // n_comp
    own = lax.dynamic_slice_in_dim(split_list[:, 0], comp * spl, spl, 0) - comp * k_dev
    src = jnp.concatenate([own, own])[None, :]
    columns = jnp.arange(k_dev, dtype=jnp.int32)
    targets = prune_list[split_list[:, 1]] - comp * k_dev
    target = (targets[:, None] == columns[None, :]).astype(bf16)
    receives = jnp.sum(target.astype(f32), 0)
    gives = jnp.sum((own[:, None] == columns[None, :]).astype(f32), 0)
    masks = jnp.stack([receives, gives])

    log_norm = math.log(npts + n_components * prior_count)
    mean_new, var_new, lw_new, send = update(sums, means, variances, src, log_norm)
    got = lax.all_to_all(
        jnp.broadcast_to(send[None], (n_comp,) + send.shape), COMP, 0, 0, tiled=True
    )
    new_means, new_variances, new_log_weights = place(
        got, target, masks, mean_new, var_new, lw_new
    )
    return new_means, new_variances, new_log_weights[0]


def solution(mesh):
    fine = Mesh(mesh.devices.reshape(4, 4, 4, 2, 2), DP + COMP)
    in_specs = (P(DP, None), P(DP, COMP), P(DP, COMP), P(COMP), P(), P())
    out_specs = (P(DP, COMP), P(DP, COMP), P(COMP))
    return jax.shard_map(
        per_device, mesh=fine, in_specs=in_specs, out_specs=out_specs, check_vma=False
    )
```

```python
import functools
import math

import jax
import jax.numpy as jnp
from jax import lax
from jax.experimental import pallas as pl
from jax.experimental.pallas import tpu as pltpu
from jax.sharding import Mesh, PartitionSpec as P

log_two_pi = math.log(2.0 * math.pi)
log_two = math.log(2.0)
prior_count = 1.0
split_scale = 0.5
extra_rows = 8
count_rows = 16
f32 = jnp.float32
bf16 = jnp.bfloat16


DP = ("zl", "y")
COMP = ("x", "zh", "c")


smem = pl.BlockSpec(memory_space=pltpu.SMEM)
vmem = pl.BlockSpec(memory_space=pltpu.VMEM)
anyspace = pl.BlockSpec(memory_space=pl.ANY)


def shape(dims, dtype=bf16):
    return jax.ShapeDtypeStruct(dims, dtype)


def call(body, out_shape, cost, limit=40, **kw):
    return pl.pallas_call(
        body,
        out_shape=out_shape,
        cost_estimate=pl.CostEstimate(
            flops=cost[0], bytes_accessed=cost[1], transcendentals=0
        ),
        compiler_params=pltpu.CompilerParams(vmem_limit_bytes=limit << 20),
        **kw,
    )


def three(value):
    high = value.astype(bf16)
    rest = value - high.astype(f32)
    mid = rest.astype(bf16)
    low = (rest - mid.astype(f32)).astype(bf16)
    return high, mid, low


def split_rows(value):
    high, mid, low = three(value)
    row = lax.broadcasted_iota(jnp.int32, (extra_rows, value.shape[1]), 0)
    return jnp.where(
        row == 0,
        high.astype(f32),
        jnp.where(row == 1, mid.astype(f32), jnp.where(row == 2, low.astype(f32), 0.0)),
    )


def join_rows(rows):
    rows = rows.astype(f32)
    return rows[0:1] + rows[1:2] + rows[2:3]


def prep_body(ids_ref, means_ref, variances_ref, out_ref):
    del ids_ref
    rows = means_ref.shape[0]
    precision = 1.0 / variances_ref[...]
    pm = precision * means_ref[...]
    out_ref[:rows, :] = pm.astype(bf16)
    out_ref[rows : 2 * rows, :] = -0.5 * precision.astype(bf16)
    partial = 0.5 * jnp.sum(jnp.log(precision), 0, keepdims=True) - 0.5 * jnp.sum(
        pm * means_ref[...], 0, keepdims=True
    )
    out_ref[2 * rows :, :] = split_rows(partial).astype(bf16)


def prep(ids, means, variances, blocks, shift):
    rows, cols = means.shape
    width = cols // blocks
    spec = pl.BlockSpec((rows, width), lambda i, ids_ref: (0, lax.rem(ids_ref[0] + shift, blocks)))
    return pl.pallas_call(
        prep_body,
        out_shape=shape((2 * rows + extra_rows, width)),
        grid_spec=pltpu.PrefetchScalarGridSpec(
            num_scalar_prefetch=1,
            grid=(1,),
            in_specs=[spec, spec],
            out_specs=pl.BlockSpec((2 * rows + extra_rows, width), lambda i, ids_ref: (0, 0)),
        ),
        name="prep",
        cost_estimate=pl.CostEstimate(
            flops=rows * width * 20, bytes_accessed=rows * width * 12, transcendentals=0
        ),
        compiler_params=pltpu.CompilerParams(vmem_limit_bytes=8 << 20),
    )(ids, means, variances)


def stack_body(*refs):
    out_ref = refs[-1]
    for i, ref in enumerate(refs[:-1]):
        out_ref[i] = ref[...]


def stack(parts):
    dims = parts[0].shape
    n = len(parts)
    return call(
        stack_body,
        shape((n,) + dims),
        (1000, 4 * n * parts[0].size),
        in_specs=[vmem] * n,
        out_specs=vmem,
    )(*parts)


def join_body(ids_ref, *refs):
    out_ref = refs[-1]
    parts = refs[:-1]
    n = len(parts)
    rows = parts[0].shape[0]
    for s, ref in enumerate(parts):
        start = lax.rem(ids_ref[0] + (n - s), n) * rows
        out_ref[pl.ds(pl.multiple_of(start, rows), rows), :] = ref[...]


def join(ids, parts):
    rows, cols = parts[0].shape
    n = len(parts)
    return call(
        join_body,
        shape((n * rows, cols)),
        (1000, 4 * n * parts[0].size),
        in_specs=[smem] + [vmem] * n,
        out_specs=vmem,
    )(ids, *parts)


def weights_body(ids_ref, logw_ref, *refs):
    wt_ref, const_ref = refs[-2:]
    ny = (len(refs) - 2) // 2
    owns = refs[:ny]
    rests = refs[ny : 2 * ny]
    nz = rests[0].shape[0] + 1
    rows, width = owns[0].shape
    rows -= extra_rows
    const = logw_ref[...]
    for t in range(ny):
        y = lax.rem(ids_ref[1] + (ny - t), ny)
        for s in range(nz):
            zl = lax.rem(ids_ref[0] + (nz - s), nz)
            part = owns[t] if s == 0 else rests[t].at[s - 1]
            start = pl.multiple_of((zl * ny + y) * rows, rows)
            wt_ref[:, pl.ds(start, rows)] = part[:rows, :].T
            const = const + join_rows(part[rows:, :])
    const_ref[...] = jnp.broadcast_to(const, (128, width)).T


def weights(ids, logw, owns, rests):
    rows, width = owns[0].shape
    depth = (rows - extra_rows) * (rests[0].shape[0] + 1) * len(owns)
    return call(
        weights_body,
        (shape((width, depth)), shape((width, 128), f32)),
        (depth * width, depth * width * 4),
        in_specs=[smem] + [vmem] * (1 + 2 * len(owns)),
        out_specs=(vmem, vmem),
    )(ids, logw, *owns, *rests)


def score_body(
    ids_ref, wt_ref, const_ref, xa_ref, xb_ref, lse_ref, score_hbm, x2_hbm, x_ref, score_ref, x2_ref, sems
):
    c = ids_ref[4]
    const = const_ref[...]
    rows, features = xa_ref.shape
    x_ref[c] = xa_ref[...]
    x_ref[1 - c] = xb_ref[...]

    def copies(half, here):
        return (
            pltpu.make_async_copy(x2_ref.at[:, here, :], x2_hbm.at[:, here, :], sems.at[0, half]),
            pltpu.make_async_copy(score_ref.at[half], score_hbm.at[half], sems.at[1, half]),
        )

    def step(half, carry):
        here = pl.ds(pl.multiple_of(half * rows, rows), rows)
        x2_copy, score_copy = copies(half, here)
        lane = lax.broadcasted_iota(jnp.int32, (rows, 128), 1)
        blocks = []
        for i in range(features // 128):
            x = x_ref[half, :, i * 128 : (i + 1) * 128].astype(f32)
            sq = (x * x).astype(bf16).astype(f32)
            first = jnp.where(lane < 64, x, pltpu.roll(sq, 64, 1)).astype(bf16)
            second = jnp.where(lane < 64, pltpu.roll(x, 64, 1), sq).astype(bf16)
            x2_ref[2 * i, here, :] = first
            x2_ref[2 * i + 1, here, :] = second
            blocks += [first, second]
        x2_copy.start()
        x2 = jnp.concatenate(blocks, axis=1)
        score = lax.dot_general(
            wt_ref[...], x2, (((1,), (1,)), ((), ())), preferred_element_type=f32
        )
        reps = -(-rows // 128)
        score = score + jnp.concatenate([const] * reps, axis=1)[:, :rows]
        score_ref[half] = score
        score_copy.start()
        top = jnp.max(score, 0, keepdims=True)
        total = jnp.sum(jnp.exp(score - top), 0, keepdims=True)
        lse = top + jnp.log(total)
        for q in range(rows // 128):
            lse_ref[pl.ds(half * (rows // 128) + q, 1), :] = lse[:, q * 128 : (q + 1) * 128]
        return carry

    lax.fori_loop(0, 2, step, 0)
    for half in range(2):
        for copy in copies(half, pl.ds(half * rows, rows)):
            copy.wait()


def scores(ids, wt, const, xa, xb):
    width, depth = wt.shape
    rows = xa.shape[0]
    return call(
        score_body,
        (
            shape((8, 128), f32),
            shape((2, width, rows), f32),
            shape((depth // 128, 2 * rows, 128)),
        ),
        (4 * width * depth * rows, width * depth * 2 + rows * depth * 6),
        in_specs=[smem] + [vmem] * 4,
        out_specs=(vmem, anyspace, anyspace),
        scratch_shapes=[
            pltpu.VMEM((2, rows, xa.shape[1]), bf16),
            pltpu.VMEM((2, width, rows), f32),
            pltpu.VMEM((depth // 128, 2 * rows, 128), bf16),
            pltpu.SemaphoreType.DMA((2, 2)),
        ],
    )(ids, wt, const, xa, xb)


def pack_body(per, ids_ref, *refs):
    mine_ref, other_ref, all_ref = refs[-3:]
    parts = refs[:-3]
    n = len(parts)
    half = mine_ref.shape[0]
    for s, ref in enumerate(parts):
        x = lax.rem(ids_ref[2] + (n - s), n)
        for q in range(per):
            all_ref[pl.ds(x * per + q, 1), :] = ref[q : q + 1, :]
    c = ids_ref[4]
    mine_ref[...] = all_ref[pl.ds(pl.multiple_of(c * half, half), half), :]
    other_ref[...] = all_ref[pl.ds(pl.multiple_of((1 - c) * half, half), half), :]


def pack(ids, parts, per):
    half = len(parts) * per // 2
    return call(
        functools.partial(pack_body, per),
        (shape((half, 128), f32), shape((half, 128), f32)),
        (1000, 40000),
        in_specs=[smem] + [vmem] * len(parts),
        out_specs=(vmem, vmem),
        scratch_shapes=[pltpu.VMEM((2 * half, 128), f32)],
    )(ids, *parts)


def spread_body(a_ref, b_ref, out_ref):
    a, b = a_ref[...], b_ref[...]
    top = jnp.maximum(a, b)
    both = top + jnp.log(jnp.exp(a - top) + jnp.exp(b - top))
    out_ref[...] = jnp.broadcast_to(both[None], out_ref.shape)


def spread(a, b, n):
    return call(
        spread_body,
        shape((n,) + a.shape, f32),
        (1000, 4 * n * a.size),
        in_specs=[vmem] * 2,
        out_specs=vmem,
    )(a, b)


def reduce_body(in_ref, out_ref):
    top = jnp.max(in_ref[...], 0)
    total = jnp.sum(jnp.exp(in_ref[...] - top[None]), 0)
    out_ref[...] = top + jnp.log(total)


def reduce(every):
    return call(
        reduce_body,
        shape(every.shape[1:], f32),
        (10 * every.size, 4 * every.size),
        in_specs=[vmem],
        out_specs=vmem,
    )(every)


def resp_body(per, ids_ref, mine_ref, other_ref, *refs):
    n = (len(refs) - 5) // 1
    parts = refs[:n]
    rt_ref, count_ref, lse_ref, buf_ref, sems = refs[n:]
    copies = []
    for s, part in enumerate(parts):
        copies.append(pltpu.make_async_copy(part, buf_ref.at[s], sems.at[s]))
        copies[-1].start()
    half = mine_ref.shape[0]
    c = ids_ref[4]
    lse_ref[pl.ds(pl.multiple_of(c * half, half), half), :] = mine_ref[...]
    lse_ref[pl.ds(pl.multiple_of((1 - c) * half, half), half), :] = other_ref[...]
    width, rows = buf_ref.shape[2:]
    step = rows // 128
    total = jnp.zeros((width, 1), f32)
    for s in range(n):
        x = lax.rem(ids_ref[2] + (n - s), n)
        copies[s].wait()
        for h in range(2):
            lse = jnp.concatenate(
                [lse_ref[pl.ds(x * per + h * step + q, 1), :] for q in range(step)], axis=1
            )
            resp = jnp.exp(buf_ref[s, h] - lse).astype(bf16)
            at = (2 * s + h) * rows
            rt_ref[:, at : at + rows] = resp
            total = total + jnp.sum(resp.astype(f32), 1, keepdims=True)
    count_ref[...] = jnp.broadcast_to(total, (width, 128)).T[0:8]


def resps(ids, mine, other, parts, per):
    _, width, rows = parts[0].shape
    n = len(parts)
    return call(
        functools.partial(resp_body, per),
        (shape((width, 2 * n * rows)), shape((8, width), f32)),
        (width * rows * n * 16, width * rows * n * 12),
        in_specs=[smem] + [vmem] * 2 + [anyspace] * n,
        out_specs=(vmem,) * 2,
        scratch_shapes=[
            pltpu.VMEM((2 * mine.shape[0], 128), f32),
            pltpu.VMEM((n, 2, width, rows), f32),
            pltpu.SemaphoreType.DMA((n,)),
        ],
    )(ids, mine, other, *parts)


def put_counts(count, out_ref, start):
    width = count.shape[1]
    pieces = []
    for part in three(count):
        for q in range(width // 128):
            pieces.append(part[:, q * 128 : (q + 1) * 128].astype(f32))
    pieces += [jnp.zeros((1, 128), f32)] * (count_rows - len(pieces))
    out_ref[start : start + count_rows, :] = jnp.concatenate(pieces, 0).astype(bf16)


def get_counts(rows, width):
    rows = rows.astype(f32)
    n = width // 128
    out = []
    for q in range(n):
        out.append(rows[q : q + 1] + rows[n + q : n + q + 1] + rows[2 * n + q : 2 * n + q + 1])
    return jnp.concatenate(out, axis=1)


def products(picks, rt_ref, parts, buf_ref, acc_ref, sems):
    rows = parts[0].shape[1]
    for i, part in enumerate(parts):
        for k, pick in enumerate(picks):
            pltpu.make_async_copy(part.at[pick], buf_ref.at[i, k], sems.at[i, k]).start()
    acc_ref[...] = jnp.zeros_like(acc_ref)

    def step(i, carry):
        for k, pick in enumerate(picks):
            pltpu.make_async_copy(parts[0].at[pick], buf_ref.at[i, k], sems.at[i, k]).wait()
        x2 = jnp.concatenate([buf_ref[i, k] for k in range(len(picks))], axis=1)
        left = rt_ref[:, pl.ds(pl.multiple_of(i * rows, rows), rows)]
        acc_ref[...] += jnp.dot(left, x2, preferred_element_type=f32)
        return carry

    lax.fori_loop(0, len(parts), step, 0)


def others(ids_ref, nz):
    return [lax.rem(ids_ref[0] + k, nz) for k in range(1, nz)]


def away_body(nz, ny, shift, ids_ref, rt_ref, count_ref, *refs):
    out_ref, buf_ref, acc, sems = refs[-4:]
    width = rt_ref.shape[0]
    y = lax.rem(ids_ref[1] + shift, ny)
    picks = [zl * ny + y for zl in others(ids_ref, nz)]
    products(picks, rt_ref, refs[:-4], buf_ref, acc, sems)
    for k in range(nz - 1):
        out_ref[k * width : (k + 1) * width, :] = acc[:, k * 128 : (k + 1) * 128].astype(bf16)
    put_counts(count_ref[0:1, :], out_ref, (nz - 1) * width)


def away(ids, rt, count, parts, nz, ny, shift):
    width = rt.shape[0]
    rows = parts[0].shape[1]
    n = len(parts)
    return call(
        functools.partial(away_body, nz, ny, shift),
        shape(((nz - 1) * width + count_rows, 128)),
        (2 * rt.size * (nz - 1) * 128, rt.size * 2 + (nz - 1) * 128 * rt.shape[1] * 2),
        in_specs=[smem] + [vmem] * 2 + [anyspace] * n,
        out_specs=vmem,
        scratch_shapes=[
            pltpu.VMEM((n, nz - 1, rows, 128), bf16),
            pltpu.VMEM((width, (nz - 1) * 128), f32),
            pltpu.SemaphoreType.DMA((n, nz - 1)),
        ],
    )(ids, rt, count, *parts)


def near_body(nz, ny, ids_ref, rt_ref, count_ref, *refs):
    n = len(refs) - ny - 4
    parts = refs[:n]
    out_refs = refs[n : n + ny]
    own_ref, buf_ref, acc, sems = refs[n + ny :]
    width = rt_ref.shape[0]
    y = ids_ref[1]
    picks = [ids_ref[0] * ny + lax.rem(y + s, ny) for s in range(ny)]
    picks += [zl * ny + y for zl in others(ids_ref, nz)]
    products(picks, rt_ref, parts, buf_ref, acc, sems)
    for s in range(ny):
        out_refs[s][...] = acc[:, s * 128 : (s + 1) * 128].astype(bf16)
    for k in range(nz - 1):
        at = (ny + k) * 128
        own_ref[k * width : (k + 1) * width, :] = acc[:, at : at + 128].astype(bf16)
    put_counts(count_ref[0:1, :], own_ref, (nz - 1) * width)


def near(ids, rt, count, parts, nz, ny):
    width = rt.shape[0]
    rows = parts[0].shape[1]
    n = len(parts)
    picks = ny + nz - 1
    return call(
        functools.partial(near_body, nz, ny),
        (shape((width, 128)),) * ny + (shape(((nz - 1) * width + count_rows, 128)),),
        (2 * rt.size * picks * 128, rt.size * 2 + picks * 128 * rt.shape[1] * 2),
        in_specs=[smem] + [vmem] * 2 + [anyspace] * n,
        out_specs=(vmem,) * (ny + 1),
        scratch_shapes=[
            pltpu.VMEM((n, picks, rows, 128), bf16),
            pltpu.VMEM((width, picks * 128), f32),
            pltpu.SemaphoreType.DMA((n, picks)),
        ],
    )(ids, rt, count, *parts)


def gather_body(ny, *refs):
    parts = refs[:ny]
    out_refs = refs[ny:-1]
    count_ref = refs[-1]
    width = out_refs[0].shape[0] - count_rows
    last = len(out_refs) * width
    count = None
    for part in parts:
        one = get_counts(part[last:, :], width)
        count = one if count is None else count + one
    count_ref[...] = jnp.broadcast_to(count, count_ref.shape)
    for k, out_ref in enumerate(out_refs):
        acc = None
        for part in parts:
            one = part[k * width : (k + 1) * width, :].astype(f32)
            acc = one if acc is None else acc + one
        out_ref[:width, :] = acc.astype(bf16)
        put_counts(count, out_ref, width)


def gather(parts, nz):
    width = (parts[0].shape[0] - count_rows) // (nz - 1)
    return call(
        functools.partial(gather_body, len(parts)),
        (shape((width + count_rows, 128)),) * (nz - 1) + (shape((8, width), f32),),
        (parts[0].size * 4, parts[0].size * 10),
        in_specs=[vmem] * len(parts),
        out_specs=(vmem,) * nz,
    )(*parts)


def update_body(log_norm, nz, ny, ids_ref, means_ref, variances_ref, src_ref, count_ref, *refs):
    mean_ref, var_ref, lw_ref, send_ref = refs[-4:]
    owns = refs[:ny]
    rests = refs[ny:-4]
    width = owns[0].shape[0]
    rows = means_ref.shape[0]
    packed = None
    for k in range(nz):
        base = pl.multiple_of(lax.rem(ids_ref[0] + (nz - k), nz) * width, width)
        cols = pl.ds(base, width)
        if k == 0:
            sums = None
            for ref in owns:
                one = ref[...].astype(f32)
                sums = one if sums is None else sums + one
            count = count_ref[0:1, :]
        else:
            sums = rests[k - 1][:width, :].astype(f32)
            count = get_counts(rests[k - 1][width:, :], width)
        sums = sums.T
        total = count + prior_count
        inverse = 1.0 / total
        means = means_ref[:, cols]
        mean_new = (sums[:rows] + prior_count * means) * inverse
        var_new = (
            sums[rows:] + prior_count * (variances_ref[:, cols] + means * means)
        ) * inverse - mean_new * mean_new
        lw_new = jnp.log(total) - log_norm
        mean_ref[:, cols] = mean_new
        var_ref[:, cols] = var_new
        lw_ref[:, cols] = jnp.broadcast_to(lw_new, (8, width))
        moved = mean_new - split_scale * jnp.sqrt(var_new)
        tail = split_rows(lw_new - log_two)
        column = lax.broadcasted_iota(jnp.int32, (width, 128), 0) + base
        lane = lax.broadcasted_iota(jnp.int32, (width, 128), 1)
        hit = column == src_ref[0:1, :]
        left = jnp.where(hit & (lane < 64), 1.0, 0.0).astype(bf16)
        right = jnp.where(hit & (lane >= 64), 1.0, 0.0).astype(bf16)
        first = jnp.concatenate([moved, tail], 0).astype(bf16)
        second = jnp.concatenate([var_new, jnp.zeros_like(tail)], 0).astype(bf16)
        one = jnp.dot(first, left, preferred_element_type=f32) + jnp.dot(
            second, right, preferred_element_type=f32
        )
        packed = one if packed is None else packed + one
    send_ref[...] = jnp.broadcast_to(packed.astype(bf16)[None], send_ref.shape)


def update(ids, means, variances, src, count, owns, rests, log_norm, n_comp):
    rows, cols = means.shape
    nz, ny = len(rests) + 1, len(owns)
    return call(
        functools.partial(update_body, log_norm, nz, ny),
        (
            shape((rows, cols), f32),
            shape((rows, cols), f32),
            shape((8, cols), f32),
            shape((n_comp, rows + extra_rows, 128)),
        ),
        (rows * cols * 300, rows * cols * 20),
        in_specs=[smem] + [vmem] * (4 + ny + nz - 1),
        out_specs=(vmem,) * 4,
    )(ids, means, variances, src, count, *owns, *rests)


def place_body(
    blocks, got_ref, target_ref, src_ref, mean_ref, var_ref, lw_ref, out_mean, out_var, out_lw
):
    owners = got_ref.shape[0]
    rows, cols = mean_ref.shape
    width = cols // blocks
    lane = lax.broadcasted_iota(jnp.int32, got_ref.shape[1:], 1)
    row = lax.broadcasted_iota(jnp.int32, got_ref.shape[1:], 0)
    firsts, seconds = [], []
    for j in range(0, owners, 2):
        one = got_ref[j].astype(f32)
        two = got_ref[j + 1].astype(f32)
        first = jnp.where(lane < 64, one, pltpu.roll(two, 64, 1))
        firsts.append(jnp.where(row == rows + 3, 1.0, first))
        seconds.append(jnp.where(lane < 64, pltpu.roll(one, 64, 1), two))
    left = jnp.concatenate(
        [jnp.concatenate(firsts, 1), jnp.concatenate(seconds, 1)], 0
    ).astype(bf16)
    ones = jnp.ones((8, 128), bf16)
    nt = (((1,), (1,)), ((), ()))
    base = rows + extra_rows
    for b in range(blocks):
        at = slice(b * width, (b + 1) * width)
        column = lax.broadcasted_iota(jnp.int32, (width, owners * 64), 0) + b * width
        hot = jnp.where(column == target_ref[0:1, :], 1.0, 0.0).astype(bf16)
        placed = lax.dot_general(left, hot, nt, preferred_element_type=f32)
        column = lax.broadcasted_iota(jnp.int32, (width, 128), 0) + b * width
        hit = jnp.where(column == src_ref[0:1, :], 0.5, 0.0).astype(bf16)
        given = lax.dot_general(ones, hit, nt, preferred_element_type=f32)[0:1]
        take = placed[rows + 3 : rows + 4] > 0.5
        mean_new = mean_ref[:, at]
        var_new = var_ref[:, at]
        moved = mean_new + given * (split_scale * jnp.sqrt(var_new))
        out_mean[:, at] = jnp.where(take, placed[:rows], moved)
        out_var[:, at] = jnp.where(take, placed[base : base + rows], var_new)
        out_lw[:, at] = jnp.where(
            take, join_rows(placed[rows : rows + 3]), lw_ref[0:1, at] - log_two * given
        )


def place(got, target, src, mean_new, var_new, lw_new, blocks):
    rows, cols = mean_new.shape
    return call(
        functools.partial(place_body, blocks),
        (shape((rows, cols), f32), shape((rows, cols), f32), shape((1, cols), f32)),
        (300 * target.size * cols, rows * cols * 16),
        in_specs=[vmem] * 6,
        out_specs=(vmem,) * 3,
    )(got, target, src, mean_new, var_new, lw_new)


def shifted(value, axis, n, s):
    return lax.ppermute(value, axis, [(i, (i + s) % n) for i in range(n)])


def per_device(points, means, variances, log_weights, split_list, prune_list):
    k_dev = means.shape[1]
    features = points.shape[1]
    n_rows = points.shape[0]
    nz, ny, nx, nc = (lax.axis_size(a) for a in ("zl", "y", "x", "c"))
    n_comp = lax.axis_size(COMP)
    zl, y, x, c = (lax.axis_index(a) for a in ("zl", "y", "x", "c"))
    comp = lax.axis_index(COMP)
    npts = n_rows * nz * ny
    n_components = k_dev * n_comp
    width = k_dev // nz
    ids = jnp.stack([zl, y, x, jnp.zeros_like(x), c]).astype(jnp.int32)

    rows = n_rows // (nx * nc)
    mine = lax.dynamic_slice_in_dim(points, (x * nc + c) * rows, rows, 0)
    sliced = [mine] + [shifted(mine, "zl", nz, s) for s in range(1, nz)]

    prepared = [prep(ids, means, variances, nz, s) for s in range(nz)]
    arrived = [shifted(prepared[s], "zl", nz, s) for s in range(1, nz)]
    owns = [prepared[0]] + [shifted(prepared[0], "y", ny, t) for t in range(1, ny)]
    sliced = lax.optimization_barrier((sliced, prepared))[0]
    joined = join(ids, sliced)
    rest = stack(arrived)
    rests = [rest] + [shifted(rest, "y", ny, t) for t in range(1, ny)]
    halves = [joined] + [shifted(joined, "x", nx, s) for s in range(1, nx)]
    pairs = [(h, shifted(h, "c", nc, 1)) for h in halves]

    spl = split_list.shape[0] // n_comp
    own = lax.dynamic_slice_in_dim(split_list[:, 0], comp * spl, spl, 0) - comp * k_dev
    src = jnp.concatenate([own, own])[None, :]
    target = (prune_list[split_list[:, 1]] - comp * k_dev)[None, :]
    logw = lax.dynamic_slice_in_dim(log_weights, zl * width, width, 0)
    logw = (logw - 0.5 * features * log_two_pi)[None, :]
    logw, src, target = lax.optimization_barrier((logw, src, target))

    wt, const = weights(ids, logw, owns, rests)
    out = [scores(ids, wt, const, a, b) for a, b in pairs]
    per = n_rows // 128
    local, away_lse = pack(ids, [o[0] for o in out], per)
    group = ("zl", "x", "zh")
    both = spread(local, shifted(away_lse, "c", nc, 1), n_comp // nc * nz)
    lse = reduce(lax.all_to_all(both, group, 0, 0, tiled=True))
    rt, count = resps(ids, lse, shifted(lse, "c", nc, 1), [o[1] for o in out], per)

    x2 = [o[2] for o in out]
    far = [None] * ny
    for t in [2, 1, 3]:
        far[t] = away(ids, rt, count, x2, nz, ny, t)
        far[t] = shifted(far[t], "y", ny, t)
    *owned, far[0] = near(ids, rt, count, x2, nz, ny)
    owned = [owned[0]] + [shifted(owned[t], "y", ny, t) for t in range(1, ny)]
    *rests, count = gather(far, nz)
    rests = [shifted(rests[k - 1], "zl", nz, k) for k in range(1, nz)]

    log_norm = math.log(npts + n_components * prior_count)
    mean_new, var_new, lw_new, send = update(
        ids, means, variances, src, count, owned, rests, log_norm, n_comp
    )
    got = lax.all_to_all(send, COMP, 0, 0, tiled=True)
    new_means, new_variances, new_log_weights = place(
        got, target, src, mean_new, var_new, lw_new, nz
    )
    return new_means, new_variances, new_log_weights[0]


def solution(mesh):
    fine = Mesh(mesh.devices.reshape(4, 4, 4, 2, 2), DP + COMP)
    in_specs = (P(DP, None), P(DP, COMP), P(DP, COMP), P(COMP), P(), P())
    out_specs = (P(DP, COMP), P(DP, COMP), P(COMP))

    return jax.shard_map(
        per_device, mesh=fine, in_specs=in_specs, out_specs=out_specs, check_vma=False
    )
```

```python
import functools
import math

import jax
import jax.numpy as jnp
from jax import lax
from jax.experimental import pallas as pl
from jax.experimental.pallas import tpu as pltpu
from jax.sharding import Mesh, PartitionSpec as P

log_two_pi = math.log(2.0 * math.pi)
log_two = math.log(2.0)
prior_count = 1.0
split_scale = 0.5
extra_rows = 8
count_rows = 16
f32 = jnp.float32
bf16 = jnp.bfloat16


DP = ("zl", "y")
COMP = ("x", "zh", "c")


smem = pl.BlockSpec(memory_space=pltpu.SMEM)
vmem = pl.BlockSpec(memory_space=pltpu.VMEM)


def shape(dims, dtype=bf16):
    return jax.ShapeDtypeStruct(dims, dtype)


def call(body, out_shape, cost, limit=24, **kw):
    return pl.pallas_call(
        body,
        out_shape=out_shape,
        cost_estimate=pl.CostEstimate(
            flops=cost[0], bytes_accessed=cost[1], transcendentals=0
        ),
        compiler_params=pltpu.CompilerParams(vmem_limit_bytes=limit << 20),
        **kw,
    )


def three(value):
    high = value.astype(bf16)
    rest = value - high.astype(f32)
    mid = rest.astype(bf16)
    low = (rest - mid.astype(f32)).astype(bf16)
    return high, mid, low


def split_rows(value):
    high, mid, low = three(value)
    row = lax.broadcasted_iota(jnp.int32, (extra_rows, value.shape[1]), 0)
    return jnp.where(
        row == 0,
        high.astype(f32),
        jnp.where(row == 1, mid.astype(f32), jnp.where(row == 2, low.astype(f32), 0.0)),
    )


def join_rows(rows):
    rows = rows.astype(f32)
    return rows[0:1] + rows[1:2] + rows[2:3]


def prep_body(ids_ref, means_ref, variances_ref, out_ref):
    del ids_ref
    rows = means_ref.shape[0]
    precision = 1.0 / variances_ref[...]
    pm = precision * means_ref[...]
    out_ref[:rows, :] = pm.astype(bf16)
    out_ref[rows : 2 * rows, :] = -0.5 * precision.astype(bf16)
    partial = 0.5 * jnp.sum(jnp.log(precision), 0, keepdims=True) - 0.5 * jnp.sum(
        pm * means_ref[...], 0, keepdims=True
    )
    out_ref[2 * rows :, :] = split_rows(partial).astype(bf16)


def prep(ids, means, variances, blocks, shift):
    rows, cols = means.shape
    width = cols // blocks
    spec = pl.BlockSpec((rows, width), lambda i, ids_ref: (0, lax.rem(ids_ref[0] + shift, blocks)))
    return pl.pallas_call(
        prep_body,
        out_shape=shape((2 * rows + extra_rows, width)),
        grid_spec=pltpu.PrefetchScalarGridSpec(
            num_scalar_prefetch=1,
            grid=(1,),
            in_specs=[spec, spec],
            out_specs=pl.BlockSpec((2 * rows + extra_rows, width), lambda i, ids_ref: (0, 0)),
        ),
        name="prep",
        cost_estimate=pl.CostEstimate(
            flops=rows * width * 20, bytes_accessed=rows * width * 12, transcendentals=0
        ),
        compiler_params=pltpu.CompilerParams(vmem_limit_bytes=8 << 20),
    )(ids, means, variances)


def stack_body(*refs):
    out_ref = refs[-1]
    for i, ref in enumerate(refs[:-1]):
        out_ref[i] = ref[...]


def stack(parts):
    dims = parts[0].shape
    n = len(parts)
    return call(
        stack_body,
        shape((n,) + dims),
        (1000, 4 * n * parts[0].size),
        in_specs=[vmem] * n,
        out_specs=vmem,
    )(*parts)


def join_body(ids_ref, *refs):
    out_ref = refs[-1]
    parts = refs[:-1]
    n = len(parts)
    rows = parts[0].shape[0]
    for s, ref in enumerate(parts):
        start = lax.rem(ids_ref[0] + (n - s), n) * rows
        out_ref[pl.ds(pl.multiple_of(start, rows), rows), :] = ref[...]


def join(ids, parts):
    rows, cols = parts[0].shape
    n = len(parts)
    return call(
        join_body,
        shape((n * rows, cols)),
        (1000, 4 * n * parts[0].size),
        in_specs=[smem] + [vmem] * n,
        out_specs=vmem,
    )(ids, *parts)


def weights_body(ids_ref, logw_ref, *refs):
    wt_ref, const_ref = refs[-2:]
    ny = (len(refs) - 2) // 2
    owns = refs[:ny]
    rests = refs[ny : 2 * ny]
    nz = rests[0].shape[0] + 1
    rows, width = owns[0].shape
    rows -= extra_rows
    const = logw_ref[...]
    for t in range(ny):
        y = lax.rem(ids_ref[1] + (ny - t), ny)
        for s in range(nz):
            zl = lax.rem(ids_ref[0] + (nz - s), nz)
            part = owns[t] if s == 0 else rests[t].at[s - 1]
            start = pl.multiple_of((zl * ny + y) * rows, rows)
            wt_ref[:, pl.ds(start, rows)] = part[:rows, :].T
            const = const + join_rows(part[rows:, :])
    const_ref[...] = jnp.broadcast_to(const, (128, width)).T


def weights(ids, logw, owns, rests):
    rows, width = owns[0].shape
    depth = (rows - extra_rows) * (rests[0].shape[0] + 1) * len(owns)
    return call(
        weights_body,
        (shape((width, depth)), shape((width, 128), f32)),
        (depth * width, depth * width * 4),
        in_specs=[smem] + [vmem] * (1 + 2 * len(owns)),
        out_specs=(vmem, vmem),
    )(ids, logw, *owns, *rests)


def score_body(ids_ref, wt_ref, const_ref, xa_ref, xb_ref, lse_ref, score_ref, x2_ref):
    c = ids_ref[4]
    const = const_ref[...]
    for half, ref in enumerate((xa_ref, xb_ref)):
        rows, features = ref.shape
        place = c if half == 0 else 1 - c
        here = pl.ds(pl.multiple_of(place * rows, rows), rows)
        lane = lax.broadcasted_iota(jnp.int32, (rows, 128), 1)
        blocks = []
        for i in range(features // 128):
            x = ref[:, i * 128 : (i + 1) * 128].astype(f32)
            sq = (x * x).astype(bf16).astype(f32)
            first = jnp.where(lane < 64, x, pltpu.roll(sq, 64, 1)).astype(bf16)
            second = jnp.where(lane < 64, pltpu.roll(x, 64, 1), sq).astype(bf16)
            x2_ref[2 * i, here, :] = first
            x2_ref[2 * i + 1, here, :] = second
            blocks += [first, second]
        x2 = jnp.concatenate(blocks, axis=1)
        score = lax.dot_general(
            wt_ref[...], x2, (((1,), (1,)), ((), ())), preferred_element_type=f32
        )
        reps = -(-rows // 128)
        score = score + jnp.concatenate([const] * reps, axis=1)[:, :rows]
        score_ref[place] = score
        top = jnp.max(score, 0, keepdims=True)
        total = jnp.sum(jnp.exp(score - top), 0, keepdims=True)
        lse = top + jnp.log(total)
        for q in range(rows // 128):
            lse_ref[pl.ds(place * (rows // 128) + q, 1), :] = lse[:, q * 128 : (q + 1) * 128]


def scores(ids, wt, const, xa, xb):
    width, depth = wt.shape
    rows = xa.shape[0]
    return call(
        score_body,
        (
            shape((8, 128), f32),
            shape((2, width, rows), f32),
            shape((depth // 128, 2 * rows, 128)),
        ),
        (4 * width * depth * rows, width * depth * 2 + rows * depth * 6),
        in_specs=[smem] + [vmem] * 4,
        out_specs=(vmem,) * 3,
    )(ids, wt, const, xa, xb)


def pack_body(per, ids_ref, *refs):
    mine_ref, other_ref, all_ref = refs[-3:]
    parts = refs[:-3]
    n = len(parts)
    half = mine_ref.shape[0]
    for s, ref in enumerate(parts):
        x = lax.rem(ids_ref[2] + (n - s), n)
        for q in range(per):
            all_ref[pl.ds(x * per + q, 1), :] = ref[q : q + 1, :]
    c = ids_ref[4]
    mine_ref[...] = all_ref[pl.ds(pl.multiple_of(c * half, half), half), :]
    other_ref[...] = all_ref[pl.ds(pl.multiple_of((1 - c) * half, half), half), :]


def pack(ids, parts, per):
    half = len(parts) * per // 2
    return call(
        functools.partial(pack_body, per),
        (shape((half, 128), f32), shape((half, 128), f32)),
        (1000, 40000),
        in_specs=[smem] + [vmem] * len(parts),
        out_specs=(vmem, vmem),
        scratch_shapes=[pltpu.VMEM((2 * half, 128), f32)],
    )(ids, *parts)


def spread_body(a_ref, b_ref, out_ref):
    a, b = a_ref[...], b_ref[...]
    top = jnp.maximum(a, b)
    both = top + jnp.log(jnp.exp(a - top) + jnp.exp(b - top))
    out_ref[...] = jnp.broadcast_to(both[None], out_ref.shape)


def spread(a, b, n):
    return call(
        spread_body,
        shape((n,) + a.shape, f32),
        (1000, 4 * n * a.size),
        in_specs=[vmem] * 2,
        out_specs=vmem,
    )(a, b)


def reduce_body(in_ref, out_ref):
    top = jnp.max(in_ref[...], 0)
    total = jnp.sum(jnp.exp(in_ref[...] - top[None]), 0)
    out_ref[...] = top + jnp.log(total)


def reduce(every):
    return call(
        reduce_body,
        shape(every.shape[1:], f32),
        (10 * every.size, 4 * every.size),
        in_specs=[vmem],
        out_specs=vmem,
    )(every)


def resp_body(per, ids_ref, mine_ref, other_ref, *refs):
    parts = refs[:-3]
    n = len(parts)
    rt_ref, count_ref, lse_ref = refs[n:]
    half = mine_ref.shape[0]
    c = ids_ref[4]
    lse_ref[pl.ds(pl.multiple_of(c * half, half), half), :] = mine_ref[...]
    lse_ref[pl.ds(pl.multiple_of((1 - c) * half, half), half), :] = other_ref[...]
    width, rows = parts[0].shape[1:]
    step = rows // 128
    total = jnp.zeros((width, 1), f32)
    for s in range(n):
        x = lax.rem(ids_ref[2] + (n - s), n)
        for h in range(2):
            lse = jnp.concatenate(
                [lse_ref[pl.ds(x * per + h * step + q, 1), :] for q in range(step)], axis=1
            )
            resp = jnp.exp(parts[s][h] - lse).astype(bf16)
            at = (2 * s + h) * rows
            rt_ref[:, at : at + rows] = resp
            total = total + jnp.sum(resp.astype(f32), 1, keepdims=True)
    count_ref[...] = jnp.broadcast_to(total, (width, 128)).T[0:8]


def resps(ids, mine, other, parts, per):
    _, width, rows = parts[0].shape
    n = len(parts)
    return call(
        functools.partial(resp_body, per),
        (shape((width, 2 * n * rows)), shape((8, width), f32)),
        (width * rows * n * 16, width * rows * n * 12),
        in_specs=[smem] + [vmem] * (2 + n),
        out_specs=(vmem,) * 2,
        scratch_shapes=[pltpu.VMEM((2 * mine.shape[0], 128), f32)],
    )(ids, mine, other, *parts)


def put_counts(count, out_ref, start):
    width = count.shape[1]
    pieces = []
    for part in three(count):
        for q in range(width // 128):
            pieces.append(part[:, q * 128 : (q + 1) * 128].astype(f32))
    pieces += [jnp.zeros((1, 128), f32)] * (count_rows - len(pieces))
    out_ref[start : start + count_rows, :] = jnp.concatenate(pieces, 0).astype(bf16)


def get_counts(rows, width):
    rows = rows.astype(f32)
    n = width // 128
    out = []
    for q in range(n):
        out.append(rows[q : q + 1] + rows[n + q : n + q + 1] + rows[2 * n + q : 2 * n + q + 1])
    return jnp.concatenate(out, axis=1)


def products(picks, rt_ref, parts):
    rows = parts[0].shape[1]
    acc = None
    for i, part in enumerate(parts):
        x2 = jnp.concatenate([part[pick] for pick in picks], axis=1)
        one = jnp.dot(rt_ref[:, i * rows : (i + 1) * rows], x2, preferred_element_type=f32)
        acc = one if acc is None else acc + one
    return acc


def others(ids_ref, nz):
    return [lax.rem(ids_ref[0] + k, nz) for k in range(1, nz)]


def away_body(nz, ny, shift, ids_ref, rt_ref, count_ref, *refs):
    out_ref = refs[-1]
    width = rt_ref.shape[0]
    y = lax.rem(ids_ref[1] + shift, ny)
    picks = [zl * ny + y for zl in others(ids_ref, nz)]
    acc = products(picks, rt_ref, refs[:-1])
    for k in range(nz - 1):
        out_ref[k * width : (k + 1) * width, :] = acc[:, k * 128 : (k + 1) * 128].astype(bf16)
    put_counts(count_ref[0:1, :], out_ref, (nz - 1) * width)


def away(ids, rt, count, parts, nz, ny, shift):
    width = rt.shape[0]
    n = len(parts)
    return call(
        functools.partial(away_body, nz, ny, shift),
        shape(((nz - 1) * width + count_rows, 128)),
        (2 * rt.size * (nz - 1) * 128, rt.size * 2 + (nz - 1) * 128 * rt.shape[1] * 2),
        in_specs=[smem] + [vmem] * (2 + n),
        out_specs=vmem,
    )(ids, rt, count, *parts)


def near_body(nz, ny, ids_ref, rt_ref, count_ref, *refs):
    n = len(refs) - ny - 1
    parts = refs[:n]
    out_refs = refs[n : n + ny]
    own_ref = refs[n + ny]
    width = rt_ref.shape[0]
    y = ids_ref[1]
    picks = [ids_ref[0] * ny + lax.rem(y + s, ny) for s in range(ny)]
    picks += [zl * ny + y for zl in others(ids_ref, nz)]
    acc = products(picks, rt_ref, parts)
    for s in range(ny):
        out_refs[s][...] = acc[:, s * 128 : (s + 1) * 128].astype(bf16)
    for k in range(nz - 1):
        at = (ny + k) * 128
        own_ref[k * width : (k + 1) * width, :] = acc[:, at : at + 128].astype(bf16)
    put_counts(count_ref[0:1, :], own_ref, (nz - 1) * width)


def near(ids, rt, count, parts, nz, ny):
    width = rt.shape[0]
    n = len(parts)
    picks = ny + nz - 1
    return call(
        functools.partial(near_body, nz, ny),
        (shape((width, 128)),) * ny + (shape(((nz - 1) * width + count_rows, 128)),),
        (2 * rt.size * picks * 128, rt.size * 2 + picks * 128 * rt.shape[1] * 2),
        in_specs=[smem] + [vmem] * (2 + n),
        out_specs=(vmem,) * (ny + 1),
    )(ids, rt, count, *parts)


def gather_body(ny, *refs):
    parts = refs[:ny]
    out_refs = refs[ny:-1]
    count_ref = refs[-1]
    width = out_refs[0].shape[0] - count_rows
    last = len(out_refs) * width
    count = None
    for part in parts:
        one = get_counts(part[last:, :], width)
        count = one if count is None else count + one
    count_ref[...] = jnp.broadcast_to(count, count_ref.shape)
    for k, out_ref in enumerate(out_refs):
        acc = None
        for part in parts:
            one = part[k * width : (k + 1) * width, :].astype(f32)
            acc = one if acc is None else acc + one
        out_ref[:width, :] = acc.astype(bf16)
        put_counts(count, out_ref, width)


def gather(parts, nz):
    width = (parts[0].shape[0] - count_rows) // (nz - 1)
    return call(
        functools.partial(gather_body, len(parts)),
        (shape((width + count_rows, 128)),) * (nz - 1) + (shape((8, width), f32),),
        (parts[0].size * 4, parts[0].size * 10),
        in_specs=[vmem] * len(parts),
        out_specs=(vmem,) * nz,
    )(*parts)


def update_body(log_norm, nz, ny, ids_ref, means_ref, variances_ref, src_ref, count_ref, *refs):
    mean_ref, var_ref, lw_ref, send_ref = refs[-4:]
    owns = refs[:ny]
    rests = refs[ny:-4]
    width = owns[0].shape[0]
    rows = means_ref.shape[0]
    packed = None
    for k in range(nz):
        base = pl.multiple_of(lax.rem(ids_ref[0] + (nz - k), nz) * width, width)
        cols = pl.ds(base, width)
        if k == 0:
            sums = None
            for ref in owns:
                one = ref[...].astype(f32)
                sums = one if sums is None else sums + one
            count = count_ref[0:1, :]
        else:
            sums = rests[k - 1][:width, :].astype(f32)
            count = get_counts(rests[k - 1][width:, :], width)
        sums = sums.T
        total = count + prior_count
        inverse = 1.0 / total
        means = means_ref[:, cols]
        mean_new = (sums[:rows] + prior_count * means) * inverse
        var_new = (
            sums[rows:] + prior_count * (variances_ref[:, cols] + means * means)
        ) * inverse - mean_new * mean_new
        lw_new = jnp.log(total) - log_norm
        mean_ref[:, cols] = mean_new
        var_ref[:, cols] = var_new
        lw_ref[:, cols] = jnp.broadcast_to(lw_new, (8, width))
        moved = mean_new - split_scale * jnp.sqrt(var_new)
        tail = split_rows(lw_new - log_two)
        column = lax.broadcasted_iota(jnp.int32, (width, 128), 0) + base
        lane = lax.broadcasted_iota(jnp.int32, (width, 128), 1)
        hit = column == src_ref[0:1, :]
        left = jnp.where(hit & (lane < 64), 1.0, 0.0).astype(bf16)
        right = jnp.where(hit & (lane >= 64), 1.0, 0.0).astype(bf16)
        first = jnp.concatenate([moved, tail], 0).astype(bf16)
        second = jnp.concatenate([var_new, jnp.zeros_like(tail)], 0).astype(bf16)
        one = jnp.dot(first, left, preferred_element_type=f32) + jnp.dot(
            second, right, preferred_element_type=f32
        )
        packed = one if packed is None else packed + one
    send_ref[...] = jnp.broadcast_to(packed.astype(bf16)[None], send_ref.shape)


def update(ids, means, variances, src, count, owns, rests, log_norm, n_comp):
    rows, cols = means.shape
    nz, ny = len(rests) + 1, len(owns)
    return call(
        functools.partial(update_body, log_norm, nz, ny),
        (
            shape((rows, cols), f32),
            shape((rows, cols), f32),
            shape((8, cols), f32),
            shape((n_comp, rows + extra_rows, 128)),
        ),
        (rows * cols * 300, rows * cols * 20),
        in_specs=[smem] + [vmem] * (4 + ny + nz - 1),
        out_specs=(vmem,) * 4,
    )(ids, means, variances, src, count, *owns, *rests)


def place_body(
    blocks, got_ref, target_ref, src_ref, mean_ref, var_ref, lw_ref, out_mean, out_var, out_lw
):
    owners = got_ref.shape[0]
    rows, cols = mean_ref.shape
    width = cols // blocks
    lane = lax.broadcasted_iota(jnp.int32, got_ref.shape[1:], 1)
    row = lax.broadcasted_iota(jnp.int32, got_ref.shape[1:], 0)
    firsts, seconds = [], []
    for j in range(0, owners, 2):
        one = got_ref[j].astype(f32)
        two = got_ref[j + 1].astype(f32)
        first = jnp.where(lane < 64, one, pltpu.roll(two, 64, 1))
        firsts.append(jnp.where(row == rows + 3, 1.0, first))
        seconds.append(jnp.where(lane < 64, pltpu.roll(one, 64, 1), two))
    left = jnp.concatenate(
        [jnp.concatenate(firsts, 1), jnp.concatenate(seconds, 1)], 0
    ).astype(bf16)
    ones = jnp.ones((8, 128), bf16)
    nt = (((1,), (1,)), ((), ()))
    base = rows + extra_rows

    def step(b, carry):
        start = pl.multiple_of(b * width, width)
        at = pl.ds(start, width)
        column = lax.broadcasted_iota(jnp.int32, (width, owners * 64), 0) + start
        hot = jnp.where(column == target_ref[0:1, :], 1.0, 0.0).astype(bf16)
        placed = lax.dot_general(left, hot, nt, preferred_element_type=f32)
        column = lax.broadcasted_iota(jnp.int32, (width, 128), 0) + start
        hit = jnp.where(column == src_ref[0:1, :], 0.5, 0.0).astype(bf16)
        given = lax.dot_general(ones, hit, nt, preferred_element_type=f32)[0:1]
        take = placed[rows + 3 : rows + 4] > 0.5
        mean_new = mean_ref[:, at]
        var_new = var_ref[:, at]
        moved = mean_new + given * (split_scale * jnp.sqrt(var_new))
        out_mean[:, at] = jnp.where(take, placed[:rows], moved)
        out_var[:, at] = jnp.where(take, placed[base : base + rows], var_new)
        out_lw[:, at] = jnp.where(
            take, join_rows(placed[rows : rows + 3]), lw_ref[0:1, at] - log_two * given
        )
        return carry

    lax.fori_loop(0, blocks, step, 0)


def place(got, target, src, mean_new, var_new, lw_new, blocks):
    rows, cols = mean_new.shape
    return call(
        functools.partial(place_body, blocks),
        (shape((rows, cols), f32), shape((rows, cols), f32), shape((1, cols), f32)),
        (300 * target.size * cols, rows * cols * 16),
        in_specs=[vmem] * 6,
        out_specs=(vmem,) * 3,
    )(got, target, src, mean_new, var_new, lw_new)


def shifted(value, axis, n, s):
    return lax.ppermute(value, axis, [(i, (i + s) % n) for i in range(n)])


def per_device(points, means, variances, log_weights, split_list, prune_list):
    k_dev = means.shape[1]
    features = points.shape[1]
    n_rows = points.shape[0]
    nz, ny, nx, nc = (lax.axis_size(a) for a in ("zl", "y", "x", "c"))
    n_comp = lax.axis_size(COMP)
    zl, y, x, c = (lax.axis_index(a) for a in ("zl", "y", "x", "c"))
    comp = lax.axis_index(COMP)
    npts = n_rows * nz * ny
    n_components = k_dev * n_comp
    width = k_dev // nz
    ids = jnp.stack([zl, y, x, jnp.zeros_like(x), c]).astype(jnp.int32)

    rows = n_rows // (nx * nc)
    mine = lax.dynamic_slice_in_dim(points, (x * nc + c) * rows, rows, 0)
    sliced = [mine] + [shifted(mine, "zl", nz, s) for s in range(1, nz)]

    prepared = [prep(ids, means, variances, nz, s) for s in range(1, nz)]
    prepared = [prep(ids, means, variances, nz, 0)] + prepared
    arrived = [shifted(prepared[s], "zl", nz, s) for s in range(1, nz)]
    owns = [prepared[0]] + [shifted(prepared[0], "y", ny, t) for t in range(1, ny)]
    sliced = lax.optimization_barrier((sliced, prepared))[0]
    joined = join(ids, sliced)
    rest = stack(arrived)
    rests = [rest] + [shifted(rest, "y", ny, t) for t in range(1, ny)]
    halves = [joined] + [shifted(joined, "x", nx, s) for s in range(1, nx)]
    pairs = [(h, shifted(h, "c", nc, 1)) for h in halves]

    spl = split_list.shape[0] // n_comp
    own = lax.dynamic_slice_in_dim(split_list[:, 0], comp * spl, spl, 0) - comp * k_dev
    src = jnp.concatenate([own, own])[None, :]
    target = (prune_list[split_list[:, 1]] - comp * k_dev)[None, :]
    logw = lax.dynamic_slice_in_dim(log_weights, zl * width, width, 0)
    logw = (logw - 0.5 * features * log_two_pi)[None, :]
    logw, src, target = lax.optimization_barrier((logw, src, target))

    wt, const = weights(ids, logw, owns, rests)
    out = [scores(ids, wt, const, a, b) for a, b in pairs]
    per = n_rows // 128
    local, away_lse = pack(ids, [o[0] for o in out], per)
    group = ("zl", "x", "zh")
    both = spread(local, shifted(away_lse, "c", nc, 1), n_comp // nc * nz)
    lse = reduce(lax.all_to_all(both, group, 0, 0, tiled=True))
    rt, count = resps(ids, lse, shifted(lse, "c", nc, 1), [o[1] for o in out], per)

    x2 = [o[2] for o in out]
    far = [None] * ny
    for t in [2, 1, 3]:
        far[t] = away(ids, rt, count, x2, nz, ny, t)
        far[t] = shifted(far[t], "y", ny, t)
    *owned, far[0] = near(ids, rt, count, x2, nz, ny)
    owned = [owned[0]] + [shifted(owned[t], "y", ny, t) for t in range(1, ny)]
    *rests, count = gather(far, nz)
    rests = [shifted(rests[k - 1], "zl", nz, k) for k in range(1, nz)]

    log_norm = math.log(npts + n_components * prior_count)
    mean_new, var_new, lw_new, send = update(
        ids, means, variances, src, count, owned, rests, log_norm, n_comp
    )
    got = lax.all_to_all(send, COMP, 0, 0, tiled=True)
    new_means, new_variances, new_log_weights = place(
        got, target, src, mean_new, var_new, lw_new, nz
    )
    return new_means, new_variances, new_log_weights[0]


def solution(mesh):
    fine = Mesh(mesh.devices.reshape(4, 4, 4, 2, 2), DP + COMP)
    in_specs = (P(DP, None), P(DP, COMP), P(DP, COMP), P(COMP), P(), P())
    out_specs = (P(DP, COMP), P(DP, COMP), P(COMP))

    return jax.shard_map(
        per_device, mesh=fine, in_specs=in_specs, out_specs=out_specs, check_vma=False
    )
```
